32 devices in a mesh: video: 2 (over y), row: 4 (over z), col: 2 (over x), sub: 2 (over core).
Axes of the slice: x: 2, y: 2, z: 4, core: 2. Of those that a mesh axis runs over, the one named last changes fastest.
Arguments:
- mid_latent: bfloat16 [4, 8, 160, 256], P('video', ('row', 'col')), parts along dimension 0, may hold values from -6 to 6
- mid_cache: bfloat16 [4, 8, 160, 256], P('video', ('row', 'col')), parts along dimension 0, may hold values from -6 to 6
- mid_kernel: bfloat16 [3, 3, 3, 256, 256], P(None, None, None, None, 'sub'), may hold values from -0.078125 to 0.078125
- mid_offset: float32 [256], P('sub'), may hold values from -3 to 3
- fine_cache: bfloat16 [4, 16, 320, 256], P('video', 'row', 'col'), parts along dimension 0, may hold values from -6 to 6
- fine_kernel: bfloat16 [3, 3, 3, 256, 256], P(None, None, None, None, 'sub'), may hold values from -0.078125 to 0.078125
- fine_offset: float32 [256], P('sub'), may hold values from -3 to 3
Outputs:
- decoded: bfloat16 [4, 16, 320, 256], P('video', 'row', 'col', 'sub'), parts along dimension 0
The draws below stay inside these ranges and needn't reach their ends.
There are 2 independent parts, one for each index of `video`. The reference program is written for one: setup_inputs(seed, part) draws one part's arguments, and reference() takes and returns one part's arrays. A program takes and returns all parts, laid end to end along the dimension named above; an argument that names none is the same for every part. Nothing has to cross between parts.
All inputs are finite; a program needn't handle non-finite values.
Results may differ from the reference program's by a relative error of at most 0.0045.
Values may be sent and summed in bfloat16 or wider, within the bound.
No kernel may reach another device: no remote copies, remote signals or barrier semaphores. Data moves between devices by JAX's collectives and lax.ppermute only.
A program may use at most 64 MiB of HBM per device.

```python
import jax
import jax.numpy as jnp
from jax import lax

C = 256
FRAMES = 2
HM = 8
MW = 160
FH = 16
FW = 320


def shard_levels(own_key, shape, cuts, smallest, high):
    gain = 1.0
    for position, blocks in cuts:
        steps = jax.random.uniform(jax.random.fold_in(jax.random.fold_in(own_key, 6), position), (blocks,), jnp.float32, smallest / len(cuts), high / len(cuts))
        gain = gain * jnp.repeat(jnp.exp(steps), shape[position] // blocks).reshape((-1,) + (1,) * (len(shape) - 1 - position))
    return gain


def gaussian(rng, extent, scale, reach, split=(), dtype=jnp.bfloat16):
    level = shard_levels(rng, extent, split, -0.22, 0.18) if split else 1.0
    values = jax.random.normal(rng, extent, jnp.float32) * scale * level
    return jnp.minimum(jnp.maximum(values, -reach), reach).astype(dtype)


def setup_inputs(seed: int = 0, part: int = 0) -> dict:
    seeds = jax.random.split(jax.random.key(seed), 8)
    part_keys = jax.random.split(jax.random.fold_in(seeds[7], part), 8)
    return {
        "mid_latent": gaussian(part_keys[0], (FRAMES, HM, MW, C), 1.0, 6.0, ((1, 8),)),
        "mid_cache": gaussian(part_keys[1], (2, HM, MW, C), 1.0, 6.0, ((1, 8),)),
        "mid_kernel": gaussian(seeds[2], (3, 3, 3, C, C), (27 * C) ** -0.5, 0.078125, ((4, 2),)),
        "mid_offset": gaussian(seeds[3], (C,), 0.5, 3.0, ((0, 2),), jnp.float32),
        "fine_cache": gaussian(part_keys[4], (2, FH, FW, C), 1.0, 6.0, ((1, 4), (2, 2))),
        "fine_kernel": gaussian(seeds[5], (3, 3, 3, C, C), (27 * C) ** -0.5, 0.078125, ((4, 2),)),
        "fine_offset": gaussian(seeds[6], (C,), 0.5, 3.0, ((0, 2),), jnp.float32),
    }


def causal_conv(frames, kernel, offset):
    field = frames.astype(jnp.float32)[None]
    result = lax.conv_general_dilated(field, kernel.astype(jnp.float32), (1, 1, 1), [(0, 0), (1, 1), (1, 1)], dimension_numbers=("NDHWC", "DHWIO", "NDHWC"), precision=lax.Precision.HIGHEST)
    return result[0] + offset


def reference(mid_latent, mid_cache, mid_kernel, mid_offset, fine_cache, fine_kernel, fine_offset):
    mid_frames = jnp.concatenate([mid_cache, mid_latent], axis=0)
    mid_out = causal_conv(mid_frames, mid_kernel, mid_offset).astype(jnp.bfloat16)
    activated = jax.nn.silu(mid_out.astype(jnp.float32)).astype(jnp.bfloat16)
    upsampled = jnp.repeat(jnp.repeat(activated, 2, axis=1), 2, axis=2)
    fine_frames = jnp.concatenate([fine_cache, upsampled], axis=0)
    return causal_conv(fine_frames, fine_kernel, fine_offset).astype(jnp.bfloat16)
```

```python
import functools

import jax
import jax.numpy as jnp
from jax import lax
from jax.experimental import pallas as pl
from jax.experimental.pallas import tpu as pltpu
from jax.sharding import PartitionSpec as P

BF16 = jnp.bfloat16
F32 = jnp.float32
PX = 16


def with_halo(x, sides, width):
    for axis, dim in sides:
        count, length = (lax.axis_size(axis), x.shape[dim])
        up = [(i, (i + 1) % count) for i in range(count - 1)]
        down = [(j, i) for i, j in up]
        last = lax.slice_in_dim(x, length - width, length, axis=dim)
        initial = lax.slice_in_dim(x, 0, width, axis=dim)
        before = lax.ppermute(last, axis, up)
        after = lax.ppermute(initial, axis, down)
        x = jnp.concatenate([before, x, after], axis=dim)
    return x


def conv_valid(frames, kernel, offset):
    result = lax.conv_general_dilated(
        frames[None],
        kernel,
        (1, 1, 1),
        "VALID",
        dimension_numbers=("NDHWC", "DHWIO", "NDHWC"),
        preferred_element_type=jnp.float32,
    )
    return (result[0] + offset).astype(jnp.bfloat16)


def double_size(field):
    return jnp.repeat(jnp.repeat(field, 2, axis=1), 2, axis=2)


def general_body(mid_latent, mid_cache, mid_kernel, mid_offset, fine_cache, fine_kernel, fine_offset):
    mid_frames = jnp.concatenate([mid_cache, mid_latent], axis=0)
    padded = with_halo(mid_frames, ((("row", "col"), 1),), 1)
    padded = jnp.pad(padded, ((0, 0), (0, 0), (1, 1), (0, 0)))
    strip_out = conv_valid(padded, mid_kernel, mid_offset)
    mid_out = lax.all_to_all(strip_out, "col", split_axis=2, concat_axis=1, tiled=True)
    gathered = lax.all_gather(mid_out, "sub", axis=3, tiled=True)
    activated = jax.nn.silu(gathered.astype(jnp.float32)).astype(jnp.bfloat16)
    upsampled = double_size(activated)
    fine_frames = with_halo(
        jnp.concatenate([fine_cache, upsampled], axis=0), (("row", 1), ("col", 2)), 1
    )
    return conv_valid(fine_frames, fine_kernel, fine_offset)


def call(body, outs, args, scratch=(), flops=0, name=None):
    vmem = pl.BlockSpec(memory_space=pltpu.VMEM)
    many = isinstance(outs, (tuple, list))
    listed = tuple(outs) if many else (outs,)
    size = sum(a.size * a.dtype.itemsize for a in args) + sum(
        o.size * o.dtype.itemsize for o in listed
    )
    return pl.pallas_call(
        body,
        out_shape=listed if many else outs,
        in_specs=[vmem] * len(args),
        out_specs=(vmem,) * len(listed) if many else vmem,
        scratch_shapes=list(scratch),
        cost_estimate=pl.CostEstimate(flops=flops, bytes_accessed=size, transcendentals=0),
        name=name,
    )(*args)


def places():
    return (
        lax.axis_index("row"),
        lax.axis_index("col"),
        lax.axis_index("sub"),
        lax.axis_size("row"),
    )


def shifted_sum(a, n):
    rows = a.shape[0]
    return (
        pltpu.roll(a[:, n : n + 128], 1, 0)
        + a[:, n + 128 : n + 256]
        + pltpu.roll(a[:, n + 256 : n + 384], rows - 1, 0)
    )


def edged_sum(a):
    rows = a.shape[0]
    at = lax.broadcasted_iota(jnp.int32, (rows, 128), 0)
    left = jnp.where(at == 0, 0.0, pltpu.roll(a[:, :128], 1, 0))
    right = jnp.where(at == rows - 1, 0.0, pltpu.roll(a[:, 256:384], rows - 1, 0))
    return left + a[:, 128:256] + right


def lanes(parts):
    return jnp.concatenate(parts, axis=1)


def stacked(parts):
    return jnp.concatenate(parts, axis=0)


def dot(a, b):
    return jnp.dot(a, b, preferred_element_type=F32)


def pack_body(strip, cache, latent, fine, own, slant, side, edge):
    _, c, s, _ = places()
    width = cache.shape[2]
    last = fine.shape[1] - 1
    here = pl.multiple_of(c * (width - strip), 8)
    there = pl.multiple_of((1 - c) * (width - strip), 8)
    near = pl.multiple_of((1 - c) * (fine.shape[2] - PX), 16)
    row = s * last
    for f in range(2):
        own[f] = cache[f, 0, pl.ds(here, strip), :]
        own[2 + f] = latent[f, 0, pl.ds(here, strip), :]
        slant[f * strip : (f + 1) * strip] = cache[f, 0, pl.ds(there, strip), :]
        slant[(2 + f) * strip : (3 + f) * strip] = latent[f, 0, pl.ds(there, strip), :]
        slant[4 * strip + PX * f : 4 * strip + PX * (f + 1)] = fine[f, row, pl.ds(near, PX), :]
        edge[f] = fine[f, row]

    @pl.when(s == 0)
    def _():
        for f in range(2):
            side[f * strip : (f + 1) * strip] = cache[f, 0, pl.ds(there, strip), :]

    @pl.when(s == 1)
    def _():
        for f in range(2):
            side[f * strip : (f + 1) * strip] = latent[f, 0, pl.ds(there, strip), :]

    for y in range(last + 1):
        side[2 * strip + PX * y : 2 * strip + PX * (y + 1)] = fine[s, y, pl.ds(near, PX), :]


def merge_body(w, out):
    def step(i, _):
        rows = pl.ds(pl.multiple_of(i * 32, 32), 32)
        for dt in (1, 2):
            k = [[w[dt, dy, dx, rows, :].astype(F32) for dx in range(3)] for dy in range(3)]
            for py, a, ys in ((0, 0, (0,)), (0, 1, (1, 2)), (1, 0, (0, 1)), (1, 1, (2,))):
                line = [functools.reduce(jnp.add, [k[y][x] for y in ys]) for x in range(3)]
                for n, v in enumerate((line[0], line[1] + line[2], line[0] + line[1], line[2])):
                    out[dt - 1, py, a, rows, n * 128 : (n + 1) * 128] = v.astype(BF16)
        return 0

    lax.fori_loop(0, w.shape[3] // 32, step, 0)


def cached_body(fine, w, acc, rows_ref):
    _, high, wide, ch = fine.shape
    for f in range(2):
        rows_ref[f, 0] = jnp.zeros((wide, ch), BF16)
        rows_ref[f, high + 1] = jnp.zeros((wide, ch), BF16)
        for y in range(high):
            rows_ref[f, y + 1] = fine[f, y]
    for t, taps in ((0, ((0, 0), (1, 1))), (1, ((1, 0),))):
        lhs = lanes(
            [
                rows_ref[f, dy : dy + high].reshape(high * wide, ch)
                for f, dt in taps
                for dy in range(3)
            ]
        )
        rhs = stacked(
            [lanes([w[dt, dy, dx] for dx in range(3)]) for f, dt in taps for dy in range(3)]
        )
        res = dot(lhs, rhs)
        for y in range(high):
            acc[t, y] = edged_sum(res[y * wide : (y + 1) * wide])


def mid_body(strip, pitch, own, side, side2, near, slant, w, w2, b, b2, out, x):
    r, c, s, rows = places()
    ch = own.shape[2]
    mine = 2 - 2 * s
    theirs = 2 * s
    inside = jnp.where(s == 0, r > 0, r < rows - 1)
    x[...] = jnp.zeros(x.shape, BF16)
    for f in range(4):
        x[f, mine + c, :strip] = own[f]
        x[f, theirs + c, :strip] = jnp.where(inside, near[f], jnp.zeros_like(near[f]))
        v = slant[f * strip : (f + 1) * strip]
        x[f, theirs + 1 - c, :strip] = jnp.where(inside, v, jnp.zeros_like(v))
    for f in range(2):
        x[2 * s + f, mine + 1 - c, :strip] = side[f * strip : (f + 1) * strip]
        x[2 - 2 * s + f, mine + 1 - c, :strip] = side2[f * strip : (f + 1) * strip]
    lhs = lanes(
        [
            stacked([x[t + dt, dy : dy + 2].reshape(2 * pitch, ch) for t in range(2)])
            for dt in range(3)
            for dy in range(3)
        ]
    )
    at = lax.broadcasted_iota(jnp.int32, (4 * pitch, 128), 0)
    block = at // pitch
    kept = at - block * pitch < strip
    outer = jnp.where(s == 0, 0, 1)
    kept = kept & (inside | (block % 2 != outer))
    for ref, bias, half in ((w, b, s), (w2, b2, 1 - s)):
        rhs = stacked(
            [lanes([ref[dt, dy, dx] for dx in range(3)]) for dt in range(3) for dy in range(3)]
        )
        v = (shifted_sum(dot(lhs, rhs), 0) + bias[...]).astype(BF16).astype(F32)
        v = v / (1.0 + jnp.exp(-v))
        out[half] = jnp.where(kept, v, 0.0).astype(BF16)


def halo_body(strip, acc, edge, edge2, side, side2, slant, corner2, w, out, blocks):
    r, c, s, rows = places()
    _, high, wide, _ = acc.shape
    out[...] = acc[...]
    for ref, v in ((edge, s), (edge2, 1 - s)):
        inside = jnp.where(v == 0, r > 0, r < rows - 1)
        dy = 2 * v
        y = (high - 1) * v
        k = [lanes([w[dt, dy, dx] for dx in range(3)]) for dt in range(2)]
        first = edged_sum(dot(lanes([ref[0], ref[1]]), stacked(k)))
        second = edged_sum(dot(ref[1], k[0]))
        out[0, y] += jnp.where(inside, first, 0.0)
        out[1, y] += jnp.where(inside, second, 0.0)
    for y in range(high):
        at = slice(2 * strip + PX * y, 2 * strip + PX * (y + 1))
        blocks[s, y + 1] = side[at]
        blocks[1 - s, y + 1] = side2[at]
    for f in range(2):
        mine = slant[4 * strip + PX * f : 4 * strip + PX * (f + 1)]
        other = corner2[PX * f : PX * (f + 1)]
        for v, p in ((s, mine), (1 - s, other)):
            inside = jnp.where(v == 0, r > 0, r < rows - 1)
            blocks[f, (high + 1) * v] = jnp.where(inside, p, jnp.zeros_like(p))
    dx = 2 - 2 * c
    at = lax.broadcasted_iota(jnp.int32, (PX, 128), 0)
    x = pl.ds(pl.multiple_of((1 - c) * (wide - PX), 16), PX)
    for t, taps in ((0, ((0, 0), (1, 1))), (1, ((1, 0),))):
        lhs = lanes(
            [
                blocks[f, dy : dy + high].reshape(high * PX, blocks.shape[3])
                for f, dt in taps
                for dy in range(3)
            ]
        )
        rhs = stacked([w[dt, dy, dx] for f, dt in taps for dy in range(3)])
        res = dot(lhs, rhs)
        for y in range(high):
            p = res[y * PX : (y + 1) * PX]
            p = jnp.where(
                c == 1,
                jnp.where(at == 0, pltpu.roll(p, 1, 0), 0.0),
                jnp.where(at == PX - 1, pltpu.roll(p, PX - 1, 0), 0.0),
            )
            out[t, y, x, :] += p


def final_body(strip, pitch, acc, act, act2, w, b, out, x, up):
    _, c, s, _ = places()
    _, high, wide, _ = acc.shape
    for ref, v in ((act, s), (act2, 1 - s)):
        for t in range(2):
            for q in range(2):
                n = (2 * t + q) * pitch
                for h in range(2):
                    x[t, 2 * v + q, :, h * 128 : (h + 1) * 128] = ref[h, n : n + pitch]
    ch = x.shape[3]
    for py in range(2):
        part = [
            lanes([x[f, py + a : py + a + 2].reshape(2 * pitch, ch) for a in range(2)])
            for f in range(2)
        ]
        main = dot(stacked(part), stacked([w[1, py, a] for a in range(2)]))
        late = dot(part[0], stacked([w[0, py, a] for a in range(2)]))
        for t in range(2):
            v = main[t * 2 * pitch : (t + 1) * 2 * pitch]
            if t == 1:
                v = v + late
            even = pltpu.roll(v[:, :128], 1, 0) + v[:, 128:256]
            odd = v[:, 256:384] + pltpu.roll(v[:, 384:], 2 * pitch - 1, 0)
            for j in range(2):
                at = slice(j * pitch, (j + 1) * pitch)
                up[t, 2 * j + py, pl.ds(0, pitch, stride=2), :] = even[at]
                up[t, 2 * j + py, pl.ds(1, pitch, stride=2), :] = odd[at]
    first = pl.multiple_of(c * 2 * (strip - wide // 2), 16)
    for t in range(2):
        for y in range(high):
            v = acc[t, y] + up[t, y, pl.ds(first, wide), :] + b[...]
            out[t, y] = v.astype(BF16)


def paired_body(mid_latent, mid_cache, mid_kernel, mid_offset, fine_cache, fine_kernel, fine_offset):
    rows = lax.axis_size("row")
    width, ch = mid_cache.shape[2:]
    high, wide = fine_cache.shape[1:3]
    strip = width // 2 + 8
    pitch = -(-strip // 16) * 16
    if pitch == strip:
        pitch += 16
    shape = jax.ShapeDtypeStruct

    def at(r, c, s):
        return (r * 2 + c) * 2 + s

    def across(cross):
        pairs = []
        for c in range(2):
            for r in range(1, rows):
                a, b = at(r, c, 0), at(r - 1, 1 - c if cross else c, 1)
                pairs += [(a, b), (b, a)]
            pairs += [(at(0, c, 0), at(0, 1 - c, 0)), (at(rows - 1, c, 1), at(rows - 1, 1 - c, 1))]
        return pairs

    def neighbour(v, cross):
        return lax.ppermute(v, ("row", "col", "sub"), across(cross))

    def swap(v, axis):
        return lax.ppermute(v, axis, [(0, 1), (1, 0)])

    kernel2 = swap(mid_kernel, "sub")
    offset2 = swap(mid_offset, "sub")
    own, slant, side, edge = call(
        functools.partial(pack_body, strip),
        (
            shape((4, strip, ch), BF16),
            shape((4 * strip + 2 * PX, ch), BF16),
            shape((2 * strip + high * PX, ch), BF16),
            shape((2, wide, ch), BF16),
        ),
        (mid_cache, mid_latent, fine_cache),
        name="pack",
    )
    slant = neighbour(slant, True)
    side = swap(side, "col")
    near = neighbour(own, False)
    edge = neighbour(edge, False)
    side2 = swap(side, "sub")
    edge2 = swap(edge, "sub")
    corner2 = swap(slant[4 * strip :], "sub")

    merged = call(
        merge_body, shape((2, 2, 2, ch, 512), BF16), (fine_kernel,), name="merge", flops=10**8
    )
    acc = call(
        cached_body,
        shape((2, high, wide, 128), F32),
        (fine_cache, fine_kernel),
        [pltpu.VMEM((2, high + 2, wide, ch), BF16)],
        flops=2 * 9 * high * wide * ch * 384,
        name="cached",
    )
    act = call(
        functools.partial(mid_body, strip, pitch),
        shape((2, 4 * pitch, 128), BF16),
        (own, side, side2, near, slant, mid_kernel, kernel2, mid_offset[None], offset2[None]),
        [pltpu.VMEM((4, 4, pitch, ch), BF16)],
        flops=2 * 9 * 4 * pitch * ch * 768,
        name="mid",
    )
    act2 = swap(act, "sub")
    acc = call(
        functools.partial(halo_body, strip),
        shape(acc.shape, F32),
        (acc, edge, edge2, side, side2, slant, corner2, fine_kernel),
        [pltpu.VMEM((2, high + 2, PX, ch), BF16)],
        flops=2 * 6 * wide * ch * 384,
        name="halo",
    )
    return call(
        functools.partial(final_body, strip, pitch),
        shape((2, high, wide, 128), BF16),
        (acc, act, act2, merged, fine_offset[None]),
        [pltpu.VMEM((2, 4, pitch, ch), BF16), pltpu.VMEM((2, high, 2 * pitch, 128), F32)],
        flops=2 * 12 * 2 * pitch * ch * 512,
        name="final",
    )


def solution(mesh):
    placed = (
        P("video", ("row", "col"), None, None),
        P("video", ("row", "col"), None, None),
        P(None, None, None, None, "sub"),
        P("sub"),
        P("video", "row", "col", None),
        P(None, None, None, None, "sub"),
        P("sub"),
    )
    sizes = mesh.shape

    def body(*args):
        paired = (
            sizes["col"] == 2
            and sizes["sub"] == 2
            and sizes["row"] > 1
            and args[0].shape[1] == 1
            and args[0].shape[2] % 16 == 0
            and args[0].shape[3] == 256
        )
        return (paired_body if paired else general_body)(*args)

    return jax.shard_map(
        body, mesh=mesh, in_specs=placed, out_specs=P("video", "row", "col", "sub"), check_vma=False
    )
```

```python
import functools

import jax
import jax.numpy as jnp
from jax import lax
from jax.experimental import pallas as pl
from jax.experimental.pallas import tpu as pltpu
from jax.sharding import PartitionSpec as P

BF16 = jnp.bfloat16
F32 = jnp.float32
GRANT = 12 * 2**20
PX = 16


def with_halo(x, sides, width):
    for axis, dim in sides:
        count, length = (lax.axis_size(axis), x.shape[dim])
        up = [(i, (i + 1) % count) for i in range(count - 1)]
        down = [(j, i) for i, j in up]
        last = lax.slice_in_dim(x, length - width, length, axis=dim)
        initial = lax.slice_in_dim(x, 0, width, axis=dim)
        before = lax.ppermute(last, axis, up)
        after = lax.ppermute(initial, axis, down)
        x = jnp.concatenate([before, x, after], axis=dim)
    return x


def conv_valid(frames, kernel, offset):
    result = lax.conv_general_dilated(
        frames[None],
        kernel,
        (1, 1, 1),
        "VALID",
        dimension_numbers=("NDHWC", "DHWIO", "NDHWC"),
        preferred_element_type=jnp.float32,
    )
    return (result[0] + offset).astype(jnp.bfloat16)


def double_size(field):
    return jnp.repeat(jnp.repeat(field, 2, axis=1), 2, axis=2)


def general_body(mid_latent, mid_cache, mid_kernel, mid_offset, fine_cache, fine_kernel, fine_offset):
    mid_frames = jnp.concatenate([mid_cache, mid_latent], axis=0)
    padded = with_halo(mid_frames, ((("row", "col"), 1),), 1)
    padded = jnp.pad(padded, ((0, 0), (0, 0), (1, 1), (0, 0)))
    strip_out = conv_valid(padded, mid_kernel, mid_offset)
    mid_out = lax.all_to_all(strip_out, "col", split_axis=2, concat_axis=1, tiled=True)
    gathered = lax.all_gather(mid_out, "sub", axis=3, tiled=True)
    activated = jax.nn.silu(gathered.astype(jnp.float32)).astype(jnp.bfloat16)
    upsampled = double_size(activated)
    fine_frames = with_halo(
        jnp.concatenate([fine_cache, upsampled], axis=0), (("row", 1), ("col", 2)), 1
    )
    return conv_valid(fine_frames, fine_kernel, fine_offset)


def call(body, outs, args, scratch=(), flops=0, name=None, space=pltpu.VMEM):
    vmem = pl.BlockSpec(memory_space=pltpu.VMEM)
    given = pl.BlockSpec(memory_space=space)
    many = isinstance(outs, (tuple, list))
    listed = tuple(outs) if many else (outs,)
    size = sum(a.size * a.dtype.itemsize for a in args) + sum(
        o.size * o.dtype.itemsize for o in listed
    )
    return pl.pallas_call(
        body,
        out_shape=listed if many else outs,
        in_specs=[given] * len(args),
        out_specs=(vmem,) * len(listed) if many else vmem,
        scratch_shapes=list(scratch),
        cost_estimate=pl.CostEstimate(flops=flops, bytes_accessed=size, transcendentals=0),
        compiler_params=pltpu.CompilerParams(vmem_limit_bytes=GRANT),
        name=name,
    )(*args)


def places():
    return (
        lax.axis_index("row"),
        lax.axis_index("col"),
        lax.axis_index("sub"),
        lax.axis_size("row"),
    )


def shifted_sum(a, n):
    rows = a.shape[0]
    return (
        pltpu.roll(a[:, n : n + 128], 1, 0)
        + a[:, n + 128 : n + 256]
        + pltpu.roll(a[:, n + 256 : n + 384], rows - 1, 0)
    )


def edged_sum(a):
    rows = a.shape[0]
    at = lax.broadcasted_iota(jnp.int32, (rows, 128), 0)
    left = jnp.where(at == 0, 0.0, pltpu.roll(a[:, :128], 1, 0))
    right = jnp.where(at == rows - 1, 0.0, pltpu.roll(a[:, 256:384], rows - 1, 0))
    return left + a[:, 128:256] + right


def lanes(parts):
    return jnp.concatenate(parts, axis=1)


def stacked(parts):
    return jnp.concatenate(parts, axis=0)


def dot(a, b):
    return jnp.dot(a, b, preferred_element_type=F32)


def pack_body(strip, cache, latent, fine, own, slant, side, edge, sems):
    _, c, s, _ = places()
    width = cache.shape[2]
    last = fine.shape[1] - 1
    here = pl.ds(pl.multiple_of(c * (width - strip), 8), strip)
    there = pl.ds(pl.multiple_of((1 - c) * (width - strip), 8), strip)
    near = pl.ds(pl.multiple_of((1 - c) * (fine.shape[2] - PX), 16), PX)
    row = s * last
    copies = []

    def copy(source, target):
        copies.append(pltpu.make_async_copy(source, target, sems.at[len(copies)]))

    for f in range(2):
        copy(cache.at[f, 0, there], slant.at[f * strip : (f + 1) * strip])
        copy(latent.at[f, 0, there], slant.at[(2 + f) * strip : (3 + f) * strip])
        copy(cache.at[f, 0, here], own.at[f])
        copy(latent.at[f, 0, here], own.at[2 + f])
        copy(fine.at[f, row, near], slant.at[4 * strip + PX * f : 4 * strip + PX * (f + 1)])
        copy(fine.at[f, row], edge.at[f])
    for y in range(last + 1):
        at = 2 * strip + PX * y
        copy(fine.at[s, y, near], side.at[at : at + PX])
    common = len(copies)
    for ref in (cache, latent):
        for f in range(2):
            copy(ref.at[f, 0, there], side.at[f * strip : (f + 1) * strip])

    for step in ("start", "wait"):
        for k in range(2):

            @pl.when(s == k)
            def _():
                for one in copies[common + 2 * k : common + 2 * k + 2]:
                    getattr(one, step)()

        for one in copies[:common]:
            getattr(one, step)()


def merge_body(w, out):
    def step(i, _):
        rows = pl.ds(pl.multiple_of(i * 32, 32), 32)
        for dt in (1, 2):
            k = [[w[dt, dy, dx, rows, :].astype(F32) for dx in range(3)] for dy in range(3)]
            for py, a, ys in ((0, 0, (0,)), (0, 1, (1, 2)), (1, 0, (0, 1)), (1, 1, (2,))):
                line = [functools.reduce(jnp.add, [k[y][x] for y in ys]) for x in range(3)]
                for n, v in enumerate((line[0], line[1] + line[2], line[0] + line[1], line[2])):
                    out[dt - 1, py, a, rows, n * 128 : (n + 1) * 128] = v.astype(BF16)
        return 0

    lax.fori_loop(0, w.shape[3] // 32, step, 0)


def cached_body(fine, w, acc, rows_ref):
    _, high, wide, ch = fine.shape
    for f in range(2):
        rows_ref[f, 0] = jnp.zeros((wide, ch), BF16)
        rows_ref[f, high + 1] = jnp.zeros((wide, ch), BF16)
        for y in range(high):
            rows_ref[f, y + 1] = fine[f, y]
    for t, taps in ((0, ((0, 0), (1, 1))), (1, ((1, 0),))):
        lhs = lanes(
            [
                rows_ref[f, dy : dy + high].reshape(high * wide, ch)
                for f, dt in taps
                for dy in range(3)
            ]
        )
        rhs = stacked(
            [lanes([w[dt, dy, dx] for dx in range(3)]) for f, dt in taps for dy in range(3)]
        )
        res = dot(lhs, rhs)
        for y in range(high):
            acc[t, y] = edged_sum(res[y * wide : (y + 1) * wide])


def mid_body(strip, pitch, own, side, side2, near, slant, w, w2, b, b2, _acc, _merged, out, x):
    r, c, s, rows = places()
    ch = own.shape[2]
    mine = 2 - 2 * s
    theirs = 2 * s
    inside = jnp.where(s == 0, r > 0, r < rows - 1)
    x[...] = jnp.zeros(x.shape, BF16)
    for f in range(4):
        x[f, mine + c, :strip] = own[f]
        x[f, theirs + c, :strip] = jnp.where(inside, near[f], jnp.zeros_like(near[f]))
        v = slant[f * strip : (f + 1) * strip]
        x[f, theirs + 1 - c, :strip] = jnp.where(inside, v, jnp.zeros_like(v))
    for f in range(2):
        x[2 * s + f, mine + 1 - c, :strip] = side[f * strip : (f + 1) * strip]
        x[2 - 2 * s + f, mine + 1 - c, :strip] = side2[f * strip : (f + 1) * strip]
    lhs = lanes(
        [
            stacked([x[t + dt, dy : dy + 2].reshape(2 * pitch, ch) for t in range(2)])
            for dt in range(3)
            for dy in range(3)
        ]
    )
    at = lax.broadcasted_iota(jnp.int32, (4 * pitch, 128), 0)
    block = at // pitch
    kept = at - block * pitch < strip
    outer = jnp.where(s == 0, 0, 1)
    kept = kept & (inside | (block % 2 != outer))
    for ref, bias, half in ((w, b, s), (w2, b2, 1 - s)):
        rhs = stacked(
            [lanes([ref[dt, dy, dx] for dx in range(3)]) for dt in range(3) for dy in range(3)]
        )
        v = (shifted_sum(dot(lhs, rhs), 0) + bias[...]).astype(BF16).astype(F32)
        v = v / (1.0 + jnp.exp(-v))
        out[half] = jnp.where(kept, v, 0.0).astype(BF16)


def halo_body(strip, acc, edge, edge2, side, side2, slant, corner2, w, out, blocks):
    r, c, s, rows = places()
    _, high, wide, _ = acc.shape
    out[...] = acc[...]
    for ref, v in ((edge, s), (edge2, 1 - s)):
        inside = jnp.where(v == 0, r > 0, r < rows - 1)
        dy = 2 * v
        y = (high - 1) * v
        k = [lanes([w[dt, dy, dx] for dx in range(3)]) for dt in range(2)]
        first = edged_sum(dot(lanes([ref[0], ref[1]]), stacked(k)))
        second = edged_sum(dot(ref[1], k[0]))
        out[0, y] += jnp.where(inside, first, 0.0)
        out[1, y] += jnp.where(inside, second, 0.0)
    for y in range(high):
        at = slice(2 * strip + PX * y, 2 * strip + PX * (y + 1))
        blocks[s, y + 1] = side[at]
        blocks[1 - s, y + 1] = side2[at]
    for f in range(2):
        mine = slant[4 * strip + PX * f : 4 * strip + PX * (f + 1)]
        other = corner2[PX * f : PX * (f + 1)]
        for v, p in ((s, mine), (1 - s, other)):
            inside = jnp.where(v == 0, r > 0, r < rows - 1)
            blocks[f, (high + 1) * v] = jnp.where(inside, p, jnp.zeros_like(p))
    dx = 2 - 2 * c
    at = lax.broadcasted_iota(jnp.int32, (PX, 128), 0)
    x = pl.ds(pl.multiple_of((1 - c) * (wide - PX), 16), PX)
    for t, taps in ((0, ((0, 0), (1, 1))), (1, ((1, 0),))):
        lhs = lanes(
            [
                blocks[f, dy : dy + high].reshape(high * PX, blocks.shape[3])
                for f, dt in taps
                for dy in range(3)
            ]
        )
        rhs = stacked([w[dt, dy, dx] for f, dt in taps for dy in range(3)])
        res = dot(lhs, rhs)
        for y in range(high):
            p = res[y * PX : (y + 1) * PX]
            p = jnp.where(
                c == 1,
                jnp.where(at == 0, pltpu.roll(p, 1, 0), 0.0),
                jnp.where(at == PX - 1, pltpu.roll(p, PX - 1, 0), 0.0),
            )
            out[t, y, x, :] += p


def final_body(strip, pitch, acc, act, act2, w, b, out, x, up):
    _, c, s, _ = places()
    _, high, wide, _ = acc.shape
    for ref, v in ((act, s), (act2, 1 - s)):
        for t in range(2):
            for q in range(2):
                n = (2 * t + q) * pitch
                for h in range(2):
                    x[t, 2 * v + q, :, h * 128 : (h + 1) * 128] = ref[h, n : n + pitch]
    ch = x.shape[3]
    for py in range(2):
        part = [
            lanes([x[f, py + a : py + a + 2].reshape(2 * pitch, ch) for a in range(2)])
            for f in range(2)
        ]
        main = dot(stacked(part), stacked([w[1, py, a] for a in range(2)]))
        late = dot(part[0], stacked([w[0, py, a] for a in range(2)]))
        for t in range(2):
            v = main[t * 2 * pitch : (t + 1) * 2 * pitch]
            if t == 1:
                v = v + late
            even = pltpu.roll(v[:, :128], 1, 0) + v[:, 128:256]
            odd = v[:, 256:384] + pltpu.roll(v[:, 384:], 2 * pitch - 1, 0)
            for j in range(2):
                at = slice(j * pitch, (j + 1) * pitch)
                up[t, 2 * j + py, pl.ds(0, pitch, stride=2), :] = even[at]
                up[t, 2 * j + py, pl.ds(1, pitch, stride=2), :] = odd[at]
    first = pl.multiple_of(c * 2 * (strip - wide // 2), 16)
    for t in range(2):
        for y in range(high):
            v = acc[t, y] + up[t, y, pl.ds(first, wide), :] + b[...]
            out[t, y] = v.astype(BF16)


def paired_body(mid_latent, mid_cache, mid_kernel, mid_offset, fine_cache, fine_kernel, fine_offset):
    rows = lax.axis_size("row")
    width, ch = mid_cache.shape[2:]
    high, wide = fine_cache.shape[1:3]
    strip = width // 2 + 8
    pitch = -(-strip // 16) * 16
    if pitch == strip:
        pitch += 16
    shape = jax.ShapeDtypeStruct

    def at(r, c, s):
        return (r * 2 + c) * 2 + s

    def across(cross):
        pairs = []
        for c in range(2):
            for r in range(1, rows):
                a, b = at(r, c, 0), at(r - 1, 1 - c if cross else c, 1)
                pairs += [(a, b), (b, a)]
            pairs += [(at(0, c, 0), at(0, 1 - c, 0)), (at(rows - 1, c, 1), at(rows - 1, 1 - c, 1))]
        return pairs

    def neighbour(v, cross):
        return lax.ppermute(v, ("row", "col", "sub"), across(cross))

    def swap(v, axis):
        return lax.ppermute(v, axis, [(0, 1), (1, 0)])

    own, slant, side, edge = call(
        functools.partial(pack_body, strip),
        (
            shape((4, strip, ch), BF16),
            shape((4 * strip + 2 * PX, ch), BF16),
            shape((2 * strip + high * PX, ch), BF16),
            shape((2, wide, ch), BF16),
        ),
        [pltpu.with_memory_space_constraint(v, pltpu.HBM) for v in (mid_cache, mid_latent, fine_cache)],
        [pltpu.SemaphoreType.DMA((2 * 6 + high + 4,))],
        name="pack",
        space=pltpu.HBM,
    )
    slant = neighbour(slant, True)
    side = swap(side, "col")
    near = neighbour(own, False)
    edge = neighbour(edge, False)
    sent, bias, own = lax.optimization_barrier((mid_kernel, mid_offset, own))
    kernel2 = swap(sent, "sub")
    offset2 = swap(bias, "sub")
    acc = call(
        cached_body,
        shape((2, high, wide, 128), F32),
        (fine_cache, fine_kernel),
        [pltpu.VMEM((2, high + 2, wide, ch), BF16)],
        flops=2 * 9 * high * wide * ch * 384,
        name="cached",
    )
    side, acc = lax.optimization_barrier((side, acc))
    side2 = swap(side, "sub")
    merged = call(
        merge_body, shape((2, 2, 2, ch, 512), BF16), (fine_kernel,), name="merge", flops=10**8
    )
    edge2 = swap(edge, "sub")
    corner2 = swap(slant[4 * strip :], "sub")
    act = call(
        functools.partial(mid_body, strip, pitch),
        shape((2, 4 * pitch, 128), BF16),
        (own, side, side2, near, slant, mid_kernel, kernel2, mid_offset[None], offset2[None], acc, merged),
        [pltpu.VMEM((4, 4, pitch, ch), BF16)],
        flops=2 * 9 * 4 * pitch * ch * 768,
        name="mid",
    )
    act2 = swap(act, "sub")
    acc = call(
        functools.partial(halo_body, strip),
        shape(acc.shape, F32),
        (acc, edge, edge2, side, side2, slant, corner2, fine_kernel),
        [pltpu.VMEM((2, high + 2, PX, ch), BF16)],
        flops=2 * 6 * wide * ch * 384,
        name="halo",
    )
    return call(
        functools.partial(final_body, strip, pitch),
        shape((2, high, wide, 128), BF16),
        (acc, act, act2, merged, fine_offset[None]),
        [pltpu.VMEM((2, 4, pitch, ch), BF16), pltpu.VMEM((2, high, 2 * pitch, 128), F32)],
        flops=2 * 12 * 2 * pitch * ch * 512,
        name="final",
    )


def solution(mesh):
    placed = (
        P("video", ("row", "col"), None, None),
        P("video", ("row", "col"), None, None),
        P(None, None, None, None, "sub"),
        P("sub"),
        P("video", "row", "col", None),
        P(None, None, None, None, "sub"),
        P("sub"),
    )
    sizes = mesh.shape

    def body(*args):
        paired = (
            sizes["col"] == 2
            and sizes["sub"] == 2
            and sizes["row"] > 1
            and args[0].shape[1] == 1
            and args[0].shape[2] % 16 == 0
            and args[0].shape[3] == 256
        )
        return (paired_body if paired else general_body)(*args)

    return jax.shard_map(
        body, mesh=mesh, in_specs=placed, out_specs=P("video", "row", "col", "sub"), check_vma=False
    )
```
